256 devices in a mesh: var: 32 (over x, z), dp: 2 (over core), segment: 4 (over y).
Axes of the slice: x: 4, y: 4, z: 8, core: 2. Of those that a mesh axis runs over, the one named last changes fastest.
Arguments:
- queries: bfloat16 [2, 4, 32, 256, 1024], P('dp', 'segment', 'var'), parts along dimension 0, may hold values from -22 to 22
- keys: bfloat16 [2, 4, 32, 256, 1024], P('dp', 'segment', 'var'), parts along dimension 0, may hold values from -22 to 22
- values: bfloat16 [2, 4, 32, 256, 1024], P('dp', 'segment', 'var'), parts along dimension 0, may hold values from -6 to 6
- out_grad: bfloat16 [2, 4, 32, 256, 1024], P('dp', 'segment', 'var'), parts along dimension 0, may hold values from -96 to 96
- proj_weight: bfloat16 [4, 2048, 3072], P('segment', 'var'), may hold values from -0.125 to 0.125
- links: int32 [32, 9], replicated, may hold values from -1 to 31, as said below
Outputs:
- passed: bfloat16 [2, 4, 32, 256, 2048], P('dp', 'segment', 'var'), parts along dimension 0
The draws below stay inside these ranges and needn't reach their ends.
There are 2 independent parts, one for each index of `dp`. The reference program is written for one: setup_inputs(seed, part) draws one part's arguments, and reference() takes and returns one part's arrays. A program takes and returns all parts, laid end to end along the dimension named above; an argument that names none is the same for every part. Nothing has to cross between parts.
Inputs may be any that keep to these rules, and one draw needn't show every extreme that they name: `links`: row v lists v itself and some of the 8 variables at cyclic distance 1 to 4 from v (indices modulo 32), each at most once, listed first in order of signed offset, the remaining entries -1; some variable lists all 9.
All inputs are finite; a program needn't handle non-finite values.
Results may differ from the reference program's by a relative error of at most 0.007.
Values may be sent and summed in bfloat16 or wider, within the bound.
A program may use at most 256 MiB of HBM per device.

```python
import math
import jax
import jax.numpy as jnp
from jax import lax

D = 2048
HEADS = 16
HS = 64
PATCHES = 256
CAUSAL_BLOCK = 128
HD = 1024
VARS = 32
SEGMENTS = 4
REACH = 4


def drawn_pair(key, part):
    root_random_key = jax.random.fold_in(key, 11)
    query_random_key, random_key_for_keys = jax.random.split(root_random_key, 2)
    full_shape = (1, SEGMENTS, VARS, PATCHES, HEADS, HS)
    query_draw = jnp.clip(jax.random.normal(query_random_key, full_shape, jnp.float32), -4.0, 4.0)
    key_draw = jnp.clip(jax.random.normal(random_key_for_keys, full_shape, jnp.float32), -4.0, 4.0)
    flat_shape = (1, SEGMENTS, VARS, PATCHES, HEADS * HS)
    return (query_draw.reshape(flat_shape), key_draw.reshape(flat_shape))


def draw_queries(key, part):
    return drawn_pair(key, part)[0].astype(jnp.bfloat16)


def draw_keys(key, part):
    return drawn_pair(key, part)[1].astype(jnp.bfloat16)


def draw_links(key, part):
    root_random_key = jax.random.fold_in(key, 5)
    key_present, key_full = jax.random.split(root_random_key, 2)
    window = 2 * REACH + 1
    offsets = jnp.arange(window, dtype=jnp.int32) - REACH
    present = jax.random.randint(key_present, (VARS, window), 0, 2)
    present = jnp.where(offsets[None, :] == 0, 1, present)
    full_row = jax.random.randint(key_full, (), 0, VARS)
    present = jnp.where(jnp.arange(VARS)[:, None] == full_row, 1, present)
    neighbor_ids = (jnp.arange(VARS, dtype=jnp.int32)[:, None] + offsets[None, :]) % VARS
    neighbor_ids = jnp.where(present == 1, neighbor_ids, -1)
    order = jnp.argsort(1 - present, axis=1, stable=True)
    return jnp.take_along_axis(neighbor_ids, order, axis=1).astype(jnp.int32)


def levels(own_key, dims, cuts, least, high):
    level = 1.0
    for axis_at, blocks in cuts:
        heights = jax.random.uniform(jax.random.fold_in(jax.random.fold_in(own_key, 6), axis_at), (blocks,), jnp.float32, least / len(cuts), high / len(cuts))
        level = level * jnp.repeat(jnp.exp(heights), dims[axis_at] // blocks).reshape((-1,) + (1,) * (len(dims) - 1 - axis_at))
    return level


def scatter_about(key, shape, scale, bound, cuts=(), kind=jnp.bfloat16):
    level = levels(key, shape, cuts, -0.22, 0.18) if cuts else 1.0
    result = jax.random.normal(key, shape, jnp.float32) * scale * level
    return jnp.minimum(jnp.maximum(result, -bound), bound).astype(kind)


def setup_inputs(seed: int = 0, part: int = 0) -> dict:
    arg_keys = jax.random.split(jax.random.key(seed), 7)
    part_keys = jax.random.split(jax.random.fold_in(arg_keys[6], part), 7)
    return {
        "queries": draw_queries(jax.random.fold_in(jax.random.fold_in(arg_keys[6], part), 71), part),
        "keys": draw_keys(jax.random.fold_in(jax.random.fold_in(arg_keys[6], part), 71), part),
        "values": scatter_about(part_keys[2], (1, SEGMENTS, VARS, PATCHES, HD), 1.0, 6.0, ((1, 4), (2, 32))),
        "out_grad": scatter_about(part_keys[3], (1, SEGMENTS, VARS, PATCHES, HD), 16.0, 96.0, ((1, 4), (2, 32))),
        "proj_weight": scatter_about(arg_keys[4], (SEGMENTS, D, 3 * HD), D ** -0.5, 0.125, ((0, 4), (1, 32))),
        "links": draw_links(jax.random.fold_in(arg_keys[6], 71), part),
    }


neg_big = -1e+30

def segment_grads(query_all, key_all, value_all, grad_all, weight, links):
    var_count, patches, feature_width = query_all.shape
    head_size = feature_width // HEADS
    score_scale = 1.0 / math.sqrt(head_size)
    token_shape = (var_count, patches, HEADS, head_size)
    query_heads = query_all.reshape(token_shape).astype(jnp.float32)
    key_heads = key_all.reshape(token_shape).astype(jnp.float32)
    value_heads = value_all.reshape(token_shape).astype(jnp.float32)
    grad_heads = grad_all.reshape(token_shape).astype(jnp.float32)
    offsets = jnp.arange(2 * REACH + 1, dtype=jnp.int32) - REACH
    block_index = jnp.arange(patches, dtype=jnp.int32) // CAUSAL_BLOCK
    causal = block_index[:, None] >= block_index[None, :]

    def one_var(carry, variable):
        key_acc, value_acc = carry
        window_ids = ((variable + offsets) % var_count).astype(jnp.int32)
        own_links = lax.dynamic_index_in_dim(links, variable, 0, keepdims=False)
        linked = jnp.any(own_links[None, :] == window_ids[:, None], axis=1)
        key_block = key_heads[window_ids]
        value_block = value_heads[window_ids]
        own_query = lax.dynamic_index_in_dim(query_heads, variable, 0, keepdims=False)
        own_grad = lax.dynamic_index_in_dim(grad_heads, variable, 0, keepdims=False)
        scores = jnp.einsum('phe,wqhe->hpwq', own_query, key_block) * score_scale
        allowed = linked[None, None, :, None] & causal[None, :, None, :]
        scores = jnp.where(allowed, scores, neg_big)
        grad_attn = jnp.einsum('phe,wqhe->hpwq', own_grad, value_block)
        row_max = scores.max(axis=(2, 3), keepdims=True)
        log_total = row_max + jnp.log(jnp.exp(scores - row_max).sum(axis=(2, 3), keepdims=True))
        attention = jnp.exp(scores - log_total)
        row_delta = (attention * grad_attn).sum(axis=(2, 3), keepdims=True)
        attention_low = lax.optimization_barrier(attention.astype(jnp.bfloat16)).astype(jnp.float32)
        score_grad = lax.optimization_barrier((score_scale * attention * (grad_attn - row_delta)).astype(jnp.bfloat16)).astype(jnp.float32)
        grad_query = jnp.einsum('hpwq,wqhe->phe', score_grad, key_block).astype(jnp.bfloat16)
        key_part = jnp.einsum('hpwq,phe->wqhe', score_grad, own_query).astype(jnp.bfloat16)
        value_part = jnp.einsum('hpwq,phe->wqhe', attention_low, own_grad).astype(jnp.bfloat16)
        key_acc = key_acc.at[window_ids].add(key_part.astype(jnp.float32))
        value_acc = value_acc.at[window_ids].add(value_part.astype(jnp.float32))
        return ((key_acc, value_acc), grad_query)
    zeros = jnp.zeros(token_shape, jnp.float32)
    (key_grad, value_grad), query_grad = lax.scan(one_var, (zeros, zeros), jnp.arange(var_count, dtype=jnp.int32))
    flat_shape = (var_count, patches, feature_width)
    qkv_grad = jnp.concatenate([query_grad.reshape(flat_shape), key_grad.astype(jnp.bfloat16).reshape(flat_shape), value_grad.astype(jnp.bfloat16).reshape(flat_shape)], axis=2)
    input_grad = jnp.dot(qkv_grad.reshape(var_count * patches, 3 * feature_width), weight.T, preferred_element_type=jnp.float32)
    return input_grad.astype(jnp.bfloat16).reshape(var_count, patches, weight.shape[0])

def reference(queries, keys, values, out_grad, proj_weight, links):

    def per_segment(segment_args):
        query_all, key_all, value_all, grad_all, weight = segment_args
        return segment_grads(query_all, key_all, value_all, grad_all, weight, links)
    input_grad = lax.map(per_segment, (queries[0], keys[0], values[0], out_grad[0], proj_weight))
    passed = jnp.concatenate([input_grad[1:], input_grad[:1]], axis=0)
    return passed[None]
```

```python
import functools
import math

import jax
import jax.numpy as jnp
from jax import lax
from jax.experimental import pallas as pl
from jax.experimental.pallas import tpu as pltpu
from jax.sharding import PartitionSpec as P

HEAD = 64
CAUSAL = 128
ROW = 8
REACH = 4
SLOTS = ROW + 2 * REACH
WINDOW = 2 * REACH + 1
PATCHES = 256
LANES = 128
MESH = pl.DeviceIdType.MESH
F32 = jnp.float32
BF16 = jnp.bfloat16
ARRIVAL = (0, 1, 7, 2, 6, 3, 5, 4)


def mod(a, n):
    return lax.rem(a + 4 * n, n)


def dot(a, b, ca, cb):
    return lax.dot_general(a, b, (((ca,), (cb,)), ((), ())), preferred_element_type=F32)


def two_heads(block, scale=None):
    if scale is not None:
        block = block * jnp.asarray(scale, block.dtype)
    first = lax.broadcasted_iota(jnp.int32, block.shape, 1) < HEAD
    zero = jnp.zeros_like(block)
    return jnp.concatenate([jnp.where(first, block, zero), jnp.where(first, zero, block)], axis=0)


def first_pass(v, refs):
    kbuf, vbuf, kT, qbuf, obuf, qc, oc, p_s, a_s, st, dkacc, dvacc, dqout = refs
    for g in range(2):
        rows = pl.ds(g * CAUSAL, CAUSAL)
        qc[g] = two_heads(qbuf[v, rows, :], 0.125)
        oc[g] = two_heads(obuf[v, rows, :])

    def one(w):
        slot = v + w
        for g in range(2):
            n = CAUSAL * (g + 1)
            s = dot(kbuf[slot, 0:n, :], qc[g], 1, 1)
            m = jnp.max(s, axis=0, keepdims=True)
            p = jnp.exp(s - m)
            a = dot(vbuf[slot, 0:n, :], oc[g], 1, 1)
            at = pl.ds(g * CAUSAL, n)
            p_s[w, at, :] = p
            a_s[w, at, :] = a
            st[0, w, g : g + 1, :] = m
            st[1, w, g : g + 1, :] = jnp.sum(p, axis=0, keepdims=True)
            st[2, w, g : g + 1, :] = jnp.sum(p * a, axis=0, keepdims=True)

    for w in range(WINDOW):
        one(w)


def second_pass(v, linked, refs):
    kbuf, vbuf, kT, qbuf, obuf, qc, oc, p_s, a_s, st, dkacc, dvacc, dqout = refs
    top = jnp.full((2, 256), -1e30, F32)
    for w in range(WINDOW):
        top = jnp.maximum(top, jnp.where(linked[w], st[0, w, 0:2, :], -1e30))
    total = jnp.zeros((2, 256), F32)
    weighted = jnp.zeros((2, 256), F32)
    for w in range(WINDOW):
        f = jnp.where(linked[w], jnp.exp(jnp.minimum(st[0, w, 0:2, :] - top, 0.0)), 0.0)
        total += f * st[1, w, 0:2, :]
        weighted += f * st[2, w, 0:2, :]
        st[0, w, 0:2, :] = f
    share = 1.0 / total
    delta = weighted * share
    st[3, 0, 0:2, :] = share
    st[3, 1, 0:2, :] = delta

    def one(w, sums):
        slot = v + w
        out = []
        parts = []
        for g in range(2):
            n = CAUSAL * (g + 1)
            at = pl.ds(g * CAUSAL, n)
            f = st[0, w, g : g + 1, :] * st[3, 0, g : g + 1, :]
            attention = p_s[w, at, :] * f
            ds = (attention * (a_s[w, at, :] - st[3, 1, g : g + 1, :])).astype(BF16)
            low = attention.astype(BF16)
            out.append(sums[g] + dot(kT[slot, :, 0:n], ds, 1, 0))
            parts.append((dot(ds, qc[g], 1, 0), dot(low, oc[g], 1, 0)))
        dkacc[slot, 0:CAUSAL, :] += parts[0][0] + parts[1][0][0:CAUSAL]
        dkacc[slot, CAUSAL:, :] += parts[1][0][CAUSAL:]
        dvacc[slot, 0:CAUSAL, :] += parts[0][1] + parts[1][1][0:CAUSAL]
        dvacc[slot, CAUSAL:, :] += parts[1][1][CAUSAL:]
        return out

    sums = [jnp.zeros((LANES, 256), F32)] * 2
    for w in range(WINDOW):
        sums = one(w, sums)
    for g in range(2):
        both = jnp.concatenate([sums[g][0:HEAD, 0:CAUSAL], sums[g][HEAD:, CAUSAL:]], axis=0)
        dqout[v, pl.ds(g * CAUSAL, CAUSAL), :] = (both.T * 0.125).astype(BF16)


def linked_row(links, gv, var_count):
    entries = [links[gv, j] for j in range(WINDOW)]
    linked = []
    for w in range(WINDOW):
        target = mod(gv + w - REACH, var_count)
        hit = entries[0] == target
        for e in entries[1:]:
            hit = jnp.logical_or(hit, e == target)
        linked.append(hit)
    return linked


def ring_order(j):
    half = (j + 1) // 2
    return REACH + half * (1 - 2 * lax.rem(j, 2))


def kernel(var_count, segments, rows_of_x, links, q_in, k_in, v_in, o_in, w_in, out,
           kbuf, vbuf, kT, qbuf, obuf, qc, oc, p_s, a_s, st, dkacc, dvacc, dqout,
           kvout, back, grads, wbuf,
           in_send, in_recv, own_sem, halo_send, halo_recv, dq_send, dq_recv,
           back_send, back_recv, kv_send, kv_recv,
           wy_send, wy_recv, wz_send, wz_recv, wx_send, wx_recv, wf_send, wf_recv, wc_send, wc_recv):
    me = lax.axis_index("var")
    core = lax.axis_index("dp")
    seg = lax.axis_index("segment")
    x, z = me // ROW, lax.rem(me, ROW)
    seg_down = mod(seg - 1, segments)
    seg_up = mod(seg + 1, segments)

    def at(xx, zz):
        return {"var": mod(xx, rows_of_x) * ROW + mod(zz, ROW)}

    def at_down(zz):
        return {"var": x * ROW + mod(zz, ROW), "segment": seg_down}

    barrier = pltpu.get_barrier_semaphore()

    def greet(where):
        pl.semaphore_signal(barrier, inc=1, device_id=where, device_id_type=MESH)

    def greet_z(d, _):
        greet(at(x, z + d))
        return 0

    def greet_y(d, _):
        greet({"var": x * ROW + mod(z + d, ROW), "segment": seg_down})
        greet({"var": x * ROW + mod(z + d, ROW), "segment": seg_up})
        return 0

    lax.fori_loop(1, ROW, greet_z, 0)
    greet(at(x + 1, z))
    greet(at(x - 1, z))
    greet({"dp": 1 - core})
    lax.fori_loop(0, ROW, greet_y, 0)
    pl.semaphore_wait(barrier, (ROW - 1) + 3 + 2 * ROW)

    def remote(src, dst, send, recv, where):
        return pltpu.make_async_remote_copy(
            src_ref=src, dst_ref=dst, send_sem=send, recv_sem=recv, device_id=where, device_id_type=MESH
        )

    def w_down():
        return remote(w_in.at[core], wbuf.at[me, core], wy_send, wy_recv, {"segment": seg_down})

    def w_var(xx, r):
        return mod(xx, rows_of_x) * ROW + mod(z - r, ROW)

    def w_z(r, step):
        ref = wbuf.at[w_var(x, r), core]
        there = (r + step) % ROW
        return remote(ref, ref, wz_send.at[there], wz_recv.at[there], at(x, z + step))

    def w_x(r, step):
        ref = wbuf.at[w_var(x, r), core]
        side = (step + 1) // 2
        return remote(ref, ref, wx_send.at[side, r], wx_recv.at[side, r], at(x + step, z))

    def w_f(r, step):
        ref = wbuf.at[w_var(x - step, r), core]
        return remote(ref, ref, wf_send.at[r], wf_recv.at[r], at(x + step, z))

    def w_c(xs, r):
        ref = wbuf.at[w_var(x + xs, r), core]
        return remote(ref, ref, wc_send.at[xs, r], wc_recv.at[xs, r], {"dp": 1 - core})

    def w_c_arrives(xs, r):
        ref = wbuf.at[w_var(x + xs, r), 1 - core]
        return remote(ref, ref, wc_send.at[xs, r], wc_recv.at[xs, r], {"dp": 1 - core})

    def w_spread(r):
        w_x(r, 1).start()
        w_x(r, -1).start()
        w_c(0, r).start()

    def w_own():
        w_down().wait_recv()
        w_z(0, 1).start()
        w_z(0, -1).start()
        w_spread(0)

    def w_z_arrived(r):
        ref = wbuf.at[w_var(x, r), core]
        remote(ref, ref, wz_send.at[r], wz_recv.at[r], at(x, z + 1)).wait_recv()
        if r in (1, 2, 3):
            w_z(r, 1).start()
        if r in (7, 6):
            w_z(r, -1).start()
        w_spread(r)

    def w_x_arrived(r):
        for step in (1, -1):
            ref = wbuf.at[w_var(x - step, r), core]
            side = (step + 1) // 2
            remote(ref, ref, wx_send.at[side, r], wx_recv.at[side, r], at(x + step, z)).wait_recv()
            if (r % 2 == 0) == (step == 1):
                w_f(r, step).start()
            w_c((-step) % 4, r).start()

    def w_f_arrived(r):
        ref = wbuf.at[w_var(x + 2, r), core]
        remote(ref, ref, wf_send.at[r], wf_recv.at[r], at(x + 1, z)).wait_recv()
        w_c(2, r).start()

    w_down().start()

    def columns(zz):
        return pl.ds(pl.multiple_of(zz * LANES, LANES), LANES)

    ins = ((k_in, kbuf, REACH), (v_in, vbuf, REACH), (q_in, qbuf, 0), (o_in, obuf, 0))

    def own(kind):
        src, dst, first = ins[kind]
        return pltpu.make_async_copy(src.at[:, columns(z)], dst.at[first + z], own_sem.at[kind])

    def to_peer(kind, d):
        src, dst, first = ins[kind]
        return remote(src.at[:, columns(mod(z + d, ROW))], dst.at[first + z],
                      in_send.at[kind, d], in_recv.at[kind, d], at(x, z + d))

    def from_peer(kind, d):
        src, dst, first = ins[kind]
        return remote(src.at[:, columns(z)], dst.at[first + mod(z - d, ROW)],
                      in_send.at[kind, d], in_recv.at[kind, d], at(x, z + d))

    for kind in range(4):
        own(kind).start()

    def send_kv(j, _):
        d = ring_order(j)
        to_peer(0, d).start()
        to_peer(1, d).start()
        return 0

    def send_qo(j, _):
        d = ring_order(6 - j)
        to_peer(2, d).start()
        to_peer(3, d).start()
        return 0

    lax.fori_loop(0, ROW - 1, send_kv, 0)
    lax.fori_loop(0, ROW - 1, send_qo, 0)
    w_own()

    def halo(kind, zs):
        buf = (kbuf, vbuf)[kind]
        up = zs // REACH
        return remote(buf.at[REACH + zs], buf.at[lax.rem(zs + 12, SLOTS)],
                      halo_send.at[kind, zs], halo_recv.at[kind, zs], at(x + 2 * up - 1, z))

    for kind in range(2):
        own(kind).wait()
        halo(kind, z).start()

    dkacc[...] = jnp.zeros_like(dkacc)
    dvacc[...] = jnp.zeros_like(dvacc)

    def take_kv(j, _):
        d = ring_order(6 - j)
        zs = mod(z - d, ROW)
        for kind in range(2):
            from_peer(kind, d).wait_recv()
            halo(kind, zs).start()
        return 0

    lax.fori_loop(0, ROW - 1, take_kv, 0)

    def turn(slot):
        kT[slot] = kbuf[slot].T

    def turn_own(j, _):
        turn(REACH + j)
        return 0

    lax.fori_loop(0, ROW, turn_own, 0)

    def take_halo(zs, _):
        slot = lax.rem(zs + 12, SLOTS)
        for kind in range(2):
            buf = (kbuf, vbuf)[kind]
            remote(buf.at[REACH + zs], buf.at[slot], halo_send.at[kind, zs], halo_recv.at[kind, zs],
                   at(x + 1, z)).wait_recv()
        turn(slot)
        return 0

    lax.fori_loop(0, ROW, take_halo, 0)
    own(2).wait()
    own(3).wait()

    refs = (kbuf, vbuf, kT, qbuf, obuf, qc, oc, p_s, a_s, st, dkacc, dvacc, dqout)

    def dq_home(d):
        return remote(dqout.at[mod(z - d, ROW)], grads.at[:, columns(z)],
                      dq_send.at[d], dq_recv.at[d], at_down(z - d))

    def step(j, _):
        d = ring_order(7 - j)
        v = mod(z - d, ROW)

        @pl.when(j > 0)
        def _():
            from_peer(2, d).wait_recv()
            from_peer(3, d).wait_recv()

        first_pass(v, refs)

        @pl.when(j > 0)
        def _():
            dq_home(ring_order(8 - j)).start()

        for when, work in {2: (1, 7), 3: (2, 6), 4: (3, 5), 5: (4,)}.items():
            @pl.when(j == when)
            def _(work=work):
                for r in work:
                    w_z_arrived(r)

        for when, work in {3: (0,), 5: (1,), 6: (7,), 7: (2,)}.items():
            @pl.when(j == when)
            def _(work=work):
                for r in work:
                    w_x_arrived(r)

        second_pass(v, linked_row(links, x * ROW + v, var_count), refs)
        return 0

    lax.fori_loop(0, ROW, step, 0)

    def out_halo(j):
        return j + ROW * (j // REACH)

    def cast_halo(j, _):
        slot = out_halo(j)
        kvout[0, slot] = dkacc[slot].astype(BF16)
        kvout[1, slot] = dvacc[slot].astype(BF16)
        return 0

    def send_back(kind, j):
        slot = out_halo(j)
        zs = lax.rem(slot + 4, SLOTS)
        up = j // REACH
        return remote(kvout.at[kind, slot], back.at[kind, zs], back_send.at[kind, zs], back_recv.at[kind, zs],
                      at(x + 2 * up - 1, z))

    lax.fori_loop(0, ROW, cast_halo, 0)

    def start_back(j, _):
        send_back(0, j).start()
        send_back(1, j).start()
        return 0

    lax.fori_loop(0, ROW, start_back, 0)
    dq_home(REACH).start()
    w_x_arrived(6)
    w_f_arrived(0)

    def from_back(kind, zs):
        return remote(kvout.at[kind, 0], back.at[kind, zs], back_send.at[kind, zs], back_recv.at[kind, zs],
                      at(x + 1, z))

    def kv_home(kind, d):
        zs = mod(z - d, ROW)
        col = pl.ds(pl.multiple_of((kind + 1) * ROW * LANES + z * LANES, LANES), LANES)
        return remote(kvout.at[kind, REACH + zs], grads.at[:, col],
                      kv_send.at[kind, d], kv_recv.at[kind, d], at_down(zs))

    def total(d):
        zs = mod(z - d, ROW)
        for kind in range(2):
            from_back(kind, zs).wait_recv()
            acc = (dkacc, dvacc)[kind]
            kvout[kind, REACH + zs] = (acc[REACH + zs] + back[kind, zs].astype(F32)).astype(BF16)

    def send_home(j, _):
        total(ring_order(j))

        @pl.when(j > 0)
        def _():
            kv_home(0, ring_order(j - 1)).start()
            kv_home(1, ring_order(j - 1)).start()

        return 0

    lax.fori_loop(0, ROW, send_home, 0)
    for r in (3, 5, 4):
        w_x_arrived(r)
        if r == 3:
            kv_home(0, 0).start()
            kv_home(1, 0).start()
    for r in ARRIVAL[1:]:
        w_f_arrived(r)

    for r in range(ROW):
        for xs in range(4):
            w_c_arrives(xs, r).wait_recv()

    def grads_arrive(d, _):
        zs = mod(z + d, ROW)
        remote(dqout.at[0], grads.at[:, columns(zs)], dq_send.at[d], dq_recv.at[d], at_down(z)).wait_recv()
        for kind in range(2):
            col = pl.ds(pl.multiple_of((kind + 1) * ROW * LANES + zs * LANES, LANES), LANES)
            remote(kvout.at[kind, 0], grads.at[:, col], kv_send.at[kind, d], kv_recv.at[kind, d],
                   at_down(z)).wait_recv()
        return 0

    lax.fori_loop(0, ROW, grads_arrive, 0)

    chunk = 4

    def project(c, _):
        w = wbuf[pl.ds(c * chunk, chunk)].reshape(chunk * 64, wbuf.shape[3])
        cols = pl.ds(pl.multiple_of(c * chunk * 64, chunk * 64), chunk * 64)
        out[:, cols] = dot(grads[...], w, 1, 1).astype(BF16)
        return 0

    lax.fori_loop(0, wbuf.shape[0] // chunk, project, 0)

    def left_z(d, _):
        for kind in range(4):
            to_peer(kind, d).wait_send()
        return 0

    lax.fori_loop(1, ROW, left_z, 0)

    def left(d, _):
        dq_home(d).wait_send()
        for kind in range(2):
            halo(kind, d).wait_send()
            kv_home(kind, d).wait_send()
            send_back(kind, d).wait_send()
        return 0

    lax.fori_loop(0, ROW, left, 0)
    w_down().wait_send()
    for r in range(ROW):
        if r in (0, 1, 2, 3):
            w_z(r, 1).wait_send()
        if r in (0, 7, 6):
            w_z(r, -1).wait_send()
        w_x(r, 1).wait_send()
        w_x(r, -1).wait_send()
        w_f(r, 1 if r % 2 == 0 else -1).wait_send()
        for xs in range(4):
            w_c(xs, r).wait_send()


def shards(queries, keys, values, out_grad, proj_weight, links):
    patches, width = queries.shape[3], queries.shape[4]
    rows, cols = proj_weight.shape[1], proj_weight.shape[2]
    var_count = lax.axis_size("var")
    segments = lax.axis_size("segment")
    rows_of_x = var_count // ROW
    dma = pltpu.SemaphoreType.DMA
    block = (PATCHES, LANES)
    passed = pl.pallas_call(
        functools.partial(kernel, var_count, segments, rows_of_x),
        out_shape=jax.ShapeDtypeStruct((patches, var_count * rows), BF16),
        in_specs=[pl.BlockSpec(memory_space=pltpu.SMEM)] + [pl.BlockSpec(memory_space=pl.ANY)] * 5,
        out_specs=pl.BlockSpec(memory_space=pltpu.VMEM),
        scratch_shapes=[
            pltpu.VMEM((SLOTS,) + block, BF16),
            pltpu.VMEM((SLOTS,) + block, BF16),
            pltpu.VMEM((SLOTS, LANES, PATCHES), BF16),
            pltpu.VMEM((ROW,) + block, BF16),
            pltpu.VMEM((ROW,) + block, BF16),
            pltpu.VMEM((2, 256, LANES), BF16),
            pltpu.VMEM((2, 256, LANES), BF16),
            pltpu.VMEM((WINDOW, 384, 256), F32),
            pltpu.VMEM((WINDOW, 384, 256), F32),
            pltpu.VMEM((4, WINDOW, 8, 256), F32),
            pltpu.VMEM((SLOTS,) + block, F32),
            pltpu.VMEM((SLOTS,) + block, F32),
            pltpu.VMEM((ROW,) + block, BF16),
            pltpu.VMEM((2, SLOTS) + block, BF16),
            pltpu.VMEM((2, ROW) + block, BF16),
            pltpu.VMEM((patches, cols), BF16),
            pltpu.VMEM((var_count, 2, rows // 2, cols), BF16),
            dma((4, ROW)), dma((4, ROW)), dma((4,)), dma((2, ROW)), dma((2, ROW)), dma((ROW,)), dma((ROW,)),
            dma((2, ROW)), dma((2, ROW)), dma((2, ROW)), dma((2, ROW)),
            dma(()), dma(()), dma((ROW,)), dma((ROW,)), dma((2, ROW)), dma((2, ROW)),
            dma((ROW,)), dma((ROW,)), dma((4, ROW)), dma((4, ROW)),
        ],
        compiler_params=pltpu.CompilerParams(
            collective_id=0, has_side_effects=True, vmem_limit_bytes=60 * 1024 * 1024
        ),
    )(
        links,
        queries.reshape(patches, width),
        keys.reshape(patches, width),
        values.reshape(patches, width),
        out_grad.reshape(patches, width),
        proj_weight.reshape(2, rows // 2, cols),
    )
    return passed.reshape(1, 1, 1, patches, var_count * rows)


def solution(mesh):
    return jax.shard_map(
        shards,
        mesh=mesh,
        in_specs=(
            P("dp", "segment", "var", None, None),
            P("dp", "segment", "var", None, None),
            P("dp", "segment", "var", None, None),
            P("dp", "segment", "var", None, None),
            P("segment", "var", None),
            P(),
        ),
        out_specs=P("dp", "segment", "var", None, None),
        check_vma=False,
    )
```

```python
import functools
import math

import jax
import jax.numpy as jnp
from jax import lax
from jax.experimental import pallas as pl
from jax.experimental.pallas import tpu as pltpu
from jax.sharding import PartitionSpec as P

HEAD = 64
CAUSAL = 128
ROW = 8
REACH = 4
SLOTS = ROW + 2 * REACH
WINDOW = 2 * REACH + 1
PATCHES = 256
LANES = 128
MESH = pl.DeviceIdType.MESH
F32 = jnp.float32
BF16 = jnp.bfloat16
ARRIVAL = (0, 1, 7, 2, 6, 3, 5, 4)


def mod(a, n):
    return lax.rem(a + 4 * n, n)


def dot(a, b, ca, cb):
    return lax.dot_general(a, b, (((ca,), (cb,)), ((), ())), preferred_element_type=F32)


def two_heads(block, scale=None):
    if scale is not None:
        block = block * jnp.asarray(scale, block.dtype)
    first = lax.broadcasted_iota(jnp.int32, block.shape, 1) < HEAD
    zero = jnp.zeros_like(block)
    return jnp.concatenate([jnp.where(first, block, zero), jnp.where(first, zero, block)], axis=0)


def first_pass(v, refs):
    kbuf, vbuf, kT, qbuf, obuf, qc, oc, p_s, a_s, st, dkacc, dvacc, dqout = refs
    for g in range(2):
        rows = pl.ds(g * CAUSAL, CAUSAL)
        qc[g] = two_heads(qbuf[v, rows, :], 0.125)
        oc[g] = two_heads(obuf[v, rows, :])

    def one(w):
        slot = v + w
        for g in range(2):
            n = CAUSAL * (g + 1)
            s = dot(kbuf[slot, 0:n, :], qc[g], 1, 1)
            m = jnp.max(s, axis=0, keepdims=True)
            p = jnp.exp(s - m)
            a = dot(vbuf[slot, 0:n, :], oc[g], 1, 1)
            at = pl.ds(g * CAUSAL, n)
            p_s[w, at, :] = p
            a_s[w, at, :] = a
            st[0, w, g : g + 1, :] = m
            st[1, w, g : g + 1, :] = jnp.sum(p, axis=0, keepdims=True)
            st[2, w, g : g + 1, :] = jnp.sum(p * a, axis=0, keepdims=True)

    for w in range(WINDOW):
        one(w)


def second_pass(v, linked, refs):
    kbuf, vbuf, kT, qbuf, obuf, qc, oc, p_s, a_s, st, dkacc, dvacc, dqout = refs
    top = jnp.full((2, 256), -1e30, F32)
    for w in range(WINDOW):
        top = jnp.maximum(top, jnp.where(linked[w], st[0, w, 0:2, :], -1e30))
    total = jnp.zeros((2, 256), F32)
    weighted = jnp.zeros((2, 256), F32)
    for w in range(WINDOW):
        f = jnp.where(linked[w], jnp.exp(jnp.minimum(st[0, w, 0:2, :] - top, 0.0)), 0.0)
        total += f * st[1, w, 0:2, :]
        weighted += f * st[2, w, 0:2, :]
        st[0, w, 0:2, :] = f
    share = 1.0 / total
    delta = weighted * share
    st[3, 0, 0:2, :] = share
    st[3, 1, 0:2, :] = delta

    def one(w, sums):
        slot = v + w
        out = []
        parts = []
        for g in range(2):
            n = CAUSAL * (g + 1)
            at = pl.ds(g * CAUSAL, n)
            f = st[0, w, g : g + 1, :] * st[3, 0, g : g + 1, :]
            attention = p_s[w, at, :] * f
            ds = (attention * (a_s[w, at, :] - st[3, 1, g : g + 1, :])).astype(BF16)
            low = attention.astype(BF16)
            out.append(sums[g] + dot(kT[slot, :, 0:n], ds, 1, 0))
            parts.append((dot(ds, qc[g], 1, 0), dot(low, oc[g], 1, 0)))
        dkacc[slot, 0:CAUSAL, :] += parts[0][0] + parts[1][0][0:CAUSAL]
        dkacc[slot, CAUSAL:, :] += parts[1][0][CAUSAL:]
        dvacc[slot, 0:CAUSAL, :] += parts[0][1] + parts[1][1][0:CAUSAL]
        dvacc[slot, CAUSAL:, :] += parts[1][1][CAUSAL:]
        return out

    sums = [jnp.zeros((LANES, 256), F32)] * 2
    for w in range(WINDOW):
        sums = one(w, sums)
    for g in range(2):
        both = jnp.concatenate([sums[g][0:HEAD, 0:CAUSAL], sums[g][HEAD:, CAUSAL:]], axis=0)
        dqout[v, pl.ds(g * CAUSAL, CAUSAL), :] = (both.T * 0.125).astype(BF16)


def linked_row(links, gv, var_count):
    entries = [links[j, gv] for j in range(WINDOW)]
    linked = []
    for w in range(WINDOW):
        target = mod(gv + w - REACH, var_count)
        hit = entries[0] == target
        for e in entries[1:]:
            hit = jnp.logical_or(hit, e == target)
        linked.append(hit)
    return linked


def ring_order(j):
    half = (j + 1) // 2
    return REACH + half * (1 - 2 * lax.rem(j, 2))


def kernel(var_count, segments, rows_of_x, links, q_in, k_in, v_in, o_in, w_in, out,
           kbuf, vbuf, kT, qbuf, obuf, qc, oc, p_s, a_s, st, dkacc, dvacc, dqout,
           kvout, back, grads, wbuf, sums, row_sem,
           in_send, in_recv, own_sem, halo_send, halo_recv, dq_send, dq_recv,
           back_send, back_recv, kv_send, kv_recv,
           wy_send, wy_recv, wz_send, wz_recv, wx_send, wx_recv, wf_send, wf_recv, wc_send, wc_recv):
    me = lax.axis_index("var")
    core = lax.axis_index("dp")
    seg = lax.axis_index("segment")
    x, z = me // ROW, lax.rem(me, ROW)
    seg_down = mod(seg - 1, segments)
    seg_up = mod(seg + 1, segments)

    def at(xx, zz):
        return {"var": mod(xx, rows_of_x) * ROW + mod(zz, ROW)}

    def at_down(zz):
        return {"var": x * ROW + mod(zz, ROW), "segment": seg_down}

    barrier = pltpu.get_barrier_semaphore()

    def greet(where):
        pl.semaphore_signal(barrier, inc=1, device_id=where, device_id_type=MESH)

    def greet_z(d, _):
        greet(at(x, z + d))
        return 0

    lax.fori_loop(1, ROW, greet_z, 0)
    greet(at(x + 1, z))
    greet(at(x - 1, z))
    greet({"dp": 1 - core})
    greet({"segment": seg_down})
    greet({"segment": seg_up})

    def columns(zz):
        return pl.ds(pl.multiple_of(zz * LANES, LANES), LANES)

    ins = ((k_in, kbuf, REACH), (v_in, vbuf, REACH), (q_in, qbuf, 0), (o_in, obuf, 0))

    def own(kind):
        src, dst, first = ins[kind]
        return pltpu.make_async_copy(src.at[:, columns(z)], dst.at[first + z], own_sem.at[kind])

    for kind in range(4):
        own(kind).start()
    dkacc[...] = jnp.zeros_like(dkacc)
    dvacc[...] = jnp.zeros_like(dvacc)
    pl.semaphore_wait(barrier, (ROW - 1) + 5)
    pl.semaphore_signal(row_sem, inc=1, device_id={"segment": seg_up}, device_id_type=MESH)

    def remote(src, dst, send, recv, where):
        return pltpu.make_async_remote_copy(
            src_ref=src, dst_ref=dst, send_sem=send, recv_sem=recv, device_id=where, device_id_type=MESH
        )

    def w_down():
        return remote(w_in.at[core], wbuf.at[me, core], wy_send, wy_recv, {"segment": seg_down})

    def w_var(xx, r):
        return mod(xx, rows_of_x) * ROW + mod(z - r, ROW)

    def w_z(r, step):
        ref = wbuf.at[w_var(x, r), core]
        there = (r + step) % ROW
        return remote(ref, ref, wz_send.at[there], wz_recv.at[there], at(x, z + step))

    def w_x(r, step):
        ref = wbuf.at[w_var(x, r), core]
        side = (step + 1) // 2
        return remote(ref, ref, wx_send.at[side, r], wx_recv.at[side, r], at(x + step, z))

    def w_f(r, step):
        ref = wbuf.at[w_var(x - step, r), core]
        return remote(ref, ref, wf_send.at[r], wf_recv.at[r], at(x + step, z))

    def w_c(xs, r):
        ref = wbuf.at[w_var(x + xs, r), core]
        return remote(ref, ref, wc_send.at[xs, r], wc_recv.at[xs, r], {"dp": 1 - core})

    def w_c_arrives(xs, r):
        ref = wbuf.at[w_var(x + xs, r), 1 - core]
        return remote(ref, ref, wc_send.at[xs, r], wc_recv.at[xs, r], {"dp": 1 - core})

    def w_spread(r):
        w_x(r, 1).start()
        w_x(r, -1).start()
        w_c(0, r).start()

    def w_own():
        w_down().wait_recv()
        w_z(0, 1).start()
        w_z(0, -1).start()
        w_spread(0)

    def w_z_arrived(r):
        ref = wbuf.at[w_var(x, r), core]
        remote(ref, ref, wz_send.at[r], wz_recv.at[r], at(x, z + 1)).wait_recv()
        if r in (1, 2, 3):
            w_z(r, 1).start()
        if r in (7, 6):
            w_z(r, -1).start()
        w_spread(r)

    def w_x_arrived(r):
        for step in (1, -1):
            ref = wbuf.at[w_var(x - step, r), core]
            side = (step + 1) // 2
            remote(ref, ref, wx_send.at[side, r], wx_recv.at[side, r], at(x + step, z)).wait_recv()
            if (r % 2 == 0) == (step == 1):
                w_f(r, step).start()
            w_c((-step) % 4, r).start()

    def w_f_arrived(r):
        ref = wbuf.at[w_var(x + 2, r), core]
        remote(ref, ref, wf_send.at[r], wf_recv.at[r], at(x + 1, z)).wait_recv()
        w_c(2, r).start()

    w_down().start()

    def to_peer(kind, d):
        src, dst, first = ins[kind]
        return remote(src.at[:, columns(mod(z + d, ROW))], dst.at[first + z],
                      in_send.at[kind, d], in_recv.at[kind, d], at(x, z + d))

    def from_peer(kind, d):
        src, dst, first = ins[kind]
        return remote(src.at[:, columns(z)], dst.at[first + mod(z - d, ROW)],
                      in_send.at[kind, d], in_recv.at[kind, d], at(x, z + d))

    def send_kv(j, _):
        d = ring_order(j)
        to_peer(0, d).start()
        to_peer(1, d).start()
        return 0

    def send_qo(j, _):
        d = ring_order(6 - j)
        to_peer(2, d).start()
        to_peer(3, d).start()
        return 0

    w_own()
    w_z_arrived(1)
    w_z_arrived(7)
    lax.fori_loop(0, ROW - 1, send_kv, 0)

    def halo(kind, zs):
        buf = (kbuf, vbuf)[kind]
        up = zs // REACH
        return remote(buf.at[REACH + zs], buf.at[lax.rem(zs + 12, SLOTS)],
                      halo_send.at[kind, zs], halo_recv.at[kind, zs], at(x + 2 * up - 1, z))

    for kind in range(2):
        own(kind).wait()
        halo(kind, z).start()

    def take_kv(j, _):
        d = ring_order(j)
        zs = mod(z - d, ROW)
        for kind in range(2):
            from_peer(kind, d).wait_recv()
            halo(kind, zs).start()
        return 0

    w_x_arrived(0)
    w_z_arrived(2)
    w_z_arrived(6)
    w_f_arrived(0)
    w_x_arrived(1)
    w_x_arrived(7)
    lax.fori_loop(0, 3, take_kv, 0)
    lax.fori_loop(0, 3, send_qo, 0)
    w_z_arrived(3)
    w_z_arrived(5)
    lax.fori_loop(3, ROW - 1, send_qo, 0)
    lax.fori_loop(3, ROW - 1, take_kv, 0)
    w_x_arrived(2)
    w_x_arrived(6)
    w_f_arrived(1)
    w_f_arrived(7)

    def turn(slot):
        kT[slot] = kbuf[slot].T

    def turn_own(j, _):
        turn(REACH + j)
        return 0

    lax.fori_loop(0, ROW, turn_own, 0)

    def take_halo(zs, _):
        slot = lax.rem(zs + 12, SLOTS)
        for kind in range(2):
            buf = (kbuf, vbuf)[kind]
            remote(buf.at[REACH + zs], buf.at[slot], halo_send.at[kind, zs], halo_recv.at[kind, zs],
                   at(x + 1, z)).wait_recv()
        turn(slot)
        return 0

    lax.fori_loop(0, ROW, take_halo, 0)
    own(2).wait()
    own(3).wait()
    pl.semaphore_wait(row_sem, 1)

    refs = (kbuf, vbuf, kT, qbuf, obuf, qc, oc, p_s, a_s, st, dkacc, dvacc, dqout)

    def dq_home(d):
        return remote(dqout.at[mod(z - d, ROW)], grads.at[:, columns(z)],
                      dq_send.at[d], dq_recv.at[d], at_down(z - d))

    def step(j, _):
        d = ring_order(7 - j)
        v = mod(z - d, ROW)

        @pl.when(j > 0)
        def _():
            from_peer(2, d).wait_recv()
            from_peer(3, d).wait_recv()

        first_pass(v, refs)

        @pl.when(j > 0)
        def _():
            dq_home(ring_order(8 - j)).start()

        plan = {
            0: [(w_z_arrived, 4)],
            2: [(w_x_arrived, 3), (w_x_arrived, 5)],
            4: [(w_f_arrived, 2), (w_f_arrived, 6), (w_x_arrived, 4)],
            6: [(w_f_arrived, 3), (w_f_arrived, 5)],
        }
        for when, work in plan.items():
            @pl.when(j == when)
            def _(work=work):
                for act, *args in work:
                    act(*args)

        second_pass(v, linked_row(links, x * ROW + v, var_count), refs)
        return 0

    lax.fori_loop(0, ROW, step, 0)

    def send_back(kind, zs):
        slot = lax.rem(zs + 12, SLOTS)
        return remote(kvout.at[kind, slot], back.at[kind, zs], back_send.at[kind, zs], back_recv.at[kind, zs],
                      at(x + 1 - 2 * (zs // REACH), z))

    def cast_halo(j, _):
        slot = lax.rem(mod(z - ring_order(j), ROW) + 12, SLOTS)
        kvout[0, slot] = dkacc[slot].astype(BF16)
        kvout[1, slot] = dvacc[slot].astype(BF16)

        @pl.when(j > 0)
        def _():
            for kind in range(2):
                send_back(kind, mod(z - ring_order(j - 1), ROW)).start()

        return 0

    lax.fori_loop(0, ROW, cast_halo, 0)
    dq_home(REACH).start()
    send_back(0, z).start()
    send_back(1, z).start()

    def from_back(kind, zs):
        return remote(kvout.at[kind, 0], back.at[kind, zs], back_send.at[kind, zs], back_recv.at[kind, zs],
                      at(x + 1, z))

    def kv_home(kind, d):
        zs = mod(z - d, ROW)
        col = pl.ds(pl.multiple_of((kind + 1) * ROW * LANES + z * LANES, LANES), LANES)
        return remote(kvout.at[kind, REACH + zs], grads.at[:, col],
                      kv_send.at[kind, d], kv_recv.at[kind, d], at_down(zs))

    def total(d):
        zs = mod(z - d, ROW)
        for kind in range(2):
            from_back(kind, zs).wait_recv()
            acc = (dkacc, dvacc)[kind]
            kvout[kind, REACH + zs] = (acc[REACH + zs] + back[kind, zs].astype(F32)).astype(BF16)

    def send_home(j, _):
        total(ring_order(j))

        @pl.when(j > 0)
        def _():
            kv_home(0, ring_order(j - 1)).start()
            kv_home(1, ring_order(j - 1)).start()

        return 0

    lax.fori_loop(0, ROW, send_home, 0)
    kv_home(0, 0).start()
    kv_home(1, 0).start()
    w_f_arrived(4)

    for r in range(ROW):
        for xs in range(4):
            w_c_arrives(xs, r).wait_recv()

    def dq_arrives(d, _):
        remote(dqout.at[0], grads.at[:, columns(mod(z + d, ROW))], dq_send.at[d], dq_recv.at[d], at_down(z)).wait_recv()
        return 0

    def kv_columns(kind, zs):
        return pl.ds(pl.multiple_of((kind + 1) * ROW * LANES + zs * LANES, LANES), LANES)

    def kv_arrives(j, _):
        d = ring_order(j)
        for kind in range(2):
            remote(kvout.at[kind, 0], grads.at[:, kv_columns(kind, mod(z + d, ROW))],
                   kv_send.at[kind, d], kv_recv.at[kind, d], at_down(z)).wait_recv()
        return 0

    chunk = 4
    width = chunk * 64

    def out_columns(c):
        return pl.ds(pl.multiple_of(c * width, width), width)

    lax.fori_loop(0, ROW, dq_arrives, 0)

    def project_q(c, _):
        w = wbuf[pl.ds(c * chunk, chunk), :, :, 0 : ROW * LANES].reshape(width, ROW * LANES)
        sums[:, out_columns(c)] = dot(grads[:, 0 : ROW * LANES], w, 1, 1)
        return 0

    lax.fori_loop(0, wbuf.shape[0] // chunk, project_q, 0)

    def project_kv(first, c):
        part = sums[:, out_columns(c)]
        for j in range(first, first + 4):
            zs = mod(z + ring_order(j), ROW)
            cols = [kv_columns(kind, zs) for kind in range(2)]
            w = [wbuf[pl.ds(c * chunk, chunk), :, :, col].reshape(width, LANES) for col in cols]
            g = [grads[:, col] for col in cols]
            part += dot(jnp.concatenate(g, axis=1), jnp.concatenate(w, axis=1), 1, 1)
        return part

    lax.fori_loop(0, 4, kv_arrives, 0)

    def project_far(c, _):
        sums[:, out_columns(c)] = project_kv(0, c)
        return 0

    lax.fori_loop(0, wbuf.shape[0] // chunk, project_far, 0)
    lax.fori_loop(4, ROW, kv_arrives, 0)

    def project_near(c, _):
        out[:, out_columns(c)] = project_kv(4, c).astype(BF16)
        return 0

    lax.fori_loop(0, wbuf.shape[0] // chunk, project_near, 0)

    def left_z(d, _):
        for kind in range(4):
            to_peer(kind, d).wait_send()
        return 0

    lax.fori_loop(1, ROW, left_z, 0)

    def left(d, _):
        dq_home(d).wait_send()
        for kind in range(2):
            halo(kind, d).wait_send()
            kv_home(kind, d).wait_send()
            send_back(kind, d).wait_send()
        return 0

    lax.fori_loop(0, ROW, left, 0)
    w_down().wait_send()
    for r in range(ROW):
        if r in (0, 1, 2, 3):
            w_z(r, 1).wait_send()
        if r in (0, 7, 6):
            w_z(r, -1).wait_send()
        w_x(r, 1).wait_send()
        w_x(r, -1).wait_send()
        w_f(r, 1 if r % 2 == 0 else -1).wait_send()
        for xs in range(4):
            w_c(xs, r).wait_send()


def shards(queries, keys, values, out_grad, proj_weight, links):
    patches, width = queries.shape[3], queries.shape[4]
    rows, cols = proj_weight.shape[1], proj_weight.shape[2]
    var_count = lax.axis_size("var")
    segments = lax.axis_size("segment")
    rows_of_x = var_count // ROW
    dma = pltpu.SemaphoreType.DMA
    block = (PATCHES, LANES)
    passed = pl.pallas_call(
        functools.partial(kernel, var_count, segments, rows_of_x),
        out_shape=jax.ShapeDtypeStruct((patches, var_count * rows), BF16),
        in_specs=[pl.BlockSpec(memory_space=pltpu.SMEM)] + [pl.BlockSpec(memory_space=pl.ANY)] * 5,
        out_specs=pl.BlockSpec(memory_space=pltpu.VMEM),
        scratch_shapes=[
            pltpu.VMEM((SLOTS,) + block, BF16),
            pltpu.VMEM((SLOTS,) + block, BF16),
            pltpu.VMEM((SLOTS, LANES, PATCHES), BF16),
            pltpu.VMEM((ROW,) + block, BF16),
            pltpu.VMEM((ROW,) + block, BF16),
            pltpu.VMEM((2, 256, LANES), BF16),
            pltpu.VMEM((2, 256, LANES), BF16),
            pltpu.VMEM((WINDOW, 384, 256), F32),
            pltpu.VMEM((WINDOW, 384, 256), F32),
            pltpu.VMEM((4, WINDOW, 8, 256), F32),
            pltpu.VMEM((SLOTS,) + block, F32),
            pltpu.VMEM((SLOTS,) + block, F32),
            pltpu.VMEM((ROW,) + block, BF16),
            pltpu.VMEM((2, SLOTS) + block, BF16),
            pltpu.VMEM((2, ROW) + block, BF16),
            pltpu.VMEM((patches, cols), BF16),
            pltpu.VMEM((var_count, 2, rows // 2, cols), BF16),
            pltpu.VMEM((patches, var_count * rows), F32),
            pltpu.SemaphoreType.REGULAR,
            dma((4, ROW)), dma((4, ROW)), dma((4,)), dma((2, ROW)), dma((2, ROW)), dma((ROW,)), dma((ROW,)),
            dma((2, ROW)), dma((2, ROW)), dma((2, ROW)), dma((2, ROW)),
            dma(()), dma(()), dma((ROW,)), dma((ROW,)), dma((2, ROW)), dma((2, ROW)),
            dma((ROW,)), dma((ROW,)), dma((4, ROW)), dma((4, ROW)),
        ],
        compiler_params=pltpu.CompilerParams(
            collective_id=0, has_side_effects=True, vmem_limit_bytes=60 * 1024 * 1024
        ),
    )(
        links.T,
        queries.reshape(patches, width),
        keys.reshape(patches, width),
        values.reshape(patches, width),
        out_grad.reshape(patches, width),
        proj_weight.reshape(2, rows // 2, cols),
    )
    return passed.reshape(1, 1, 1, patches, var_count * rows)


def solution(mesh):
    return jax.shard_map(
        shards,
        mesh=mesh,
        in_specs=(
            P("dp", "segment", "var", None, None),
            P("dp", "segment", "var", None, None),
            P("dp", "segment", "var", None, None),
            P("dp", "segment", "var", None, None),
            P("segment", "var", None),
            P(),
        ),
        out_specs=P("dp", "segment", "var", None, None),
        check_vma=False,
    )
```
